32 devices in a mesh: parts: 2 (over y), ctx: 4 (over z), head: 2 (over x), sub: 2 (over core).
Axes of the slice: x: 2, y: 2, z: 4, core: 2. Of those that a mesh axis runs over, the one named last changes fastest.
Arguments:
- queries: bfloat16 [4096, 4096], P(('parts', 'ctx', 'head', 'sub')), parts along dimension 0, may hold values from -6 to 6
- keys: bfloat16 [4096, 4096], P(('parts', 'ctx', 'head', 'sub')), parts along dimension 0, may hold values from -6 to 6
- values: bfloat16 [4096, 4096], P(('parts', 'ctx', 'head', 'sub')), parts along dimension 0, may hold values from -6 to 6
Outputs:
- attended: bfloat16 [4096, 4096], P(('parts', 'ctx', 'head', 'sub')), parts along dimension 0
The draws below stay inside these ranges and needn't reach their ends.
There are 2 independent parts, one for each index of `parts`. The reference program is written for one: setup_inputs(seed, part) draws one part's arguments, and reference() takes and returns one part's arrays. A program takes and returns all parts, laid end to end along the dimension named above; each array names one. Nothing has to cross between parts.
All inputs are finite; a program needn't handle non-finite values.
Results may differ from the reference program's by a relative error of at most 0.006.
Values may be sent and summed in bfloat16 or wider, within the bound.
A program may use at most 64 MiB of HBM per device.

```python
import jax
import jax.numpy as jnp
from jax import lax

HEADS = 32
HD = 128
D = 4096
TOKENS = 2048


def level_of(own_key, shape, pieces, smallest, largest):
    def one(axis_at, shards_of):
        draws = jax.random.uniform(jax.random.fold_in(jax.random.fold_in(own_key, 6), axis_at), (shards_of,), jnp.float32, smallest / len(pieces), largest / len(pieces))
        return jnp.repeat(jnp.exp(draws), shape[axis_at] // shards_of).reshape((-1,) + (1,) * (len(shape) - axis_at - 1))

    factor_of = one(*pieces[0])
    for cut in pieces[1:]:
        factor_of = factor_of * one(*cut)
    return factor_of


def gaussian(stream_key, dims, deviation, reach, pieces=(), kind=jnp.bfloat16):
    drawn = jax.random.normal(stream_key, dims, jnp.float32) * deviation
    if len(pieces) > 0:
        drawn = level_of(stream_key, dims, pieces, -0.22, 0.18) * drawn
    return jnp.clip(drawn, min=-reach, max=reach).astype(kind)


def setup_inputs(seed: int = 0, part: int = 0) -> dict:
    seeds = jax.random.split(jax.random.key(seed), 4)
    part_splits = jax.random.split(jax.random.fold_in(seeds[3], part), 4)
    return {
        "queries": gaussian(part_splits[0], (TOKENS, D), 1.0, 6.0, ((0, 16),)),
        "keys": gaussian(part_splits[1], (TOKENS, D), 1.0, 6.0, ((0, 16),)),
        "values": gaussian(part_splits[2], (TOKENS, D), 1.0, 6.0, ((0, 16),)),
    }


def feature(x):
    return (jax.nn.elu(x.astype(jnp.float32)) + 1.0).astype(jnp.bfloat16)

def one_head(args):
    phi_q, phi_k, vals = args
    rows = 128
    count = TOKENS // rows
    qb = phi_q.reshape(count, rows, HD)
    kb = phi_k.reshape(count, rows, HD)
    vb = vals.reshape(count, rows, HD)
    causal = jnp.tril(jnp.ones((rows, rows), jnp.float32))

    def step(state, blk):
        qq, kk, vv = blk
        inter = jnp.dot(qq.astype(jnp.float32), state, precision=lax.Precision.HIGHEST)
        scores = jnp.dot(qq, kk.T, preferred_element_type=jnp.float32) * causal
        intra = jnp.dot(scores, vv.astype(jnp.float32), precision=lax.Precision.HIGHEST)
        state = state + jnp.dot(kk.T, vv, preferred_element_type=jnp.float32)
        return (state, inter + intra)
    init = jnp.zeros((HD, HD), jnp.float32)
    final, numer = lax.scan(step, init, (qb, kb, vb))
    numer = numer.reshape(TOKENS, HD)
    scaled = numer * lax.rsqrt(lax.optimization_barrier(jnp.mean(numer * numer, axis=-1, keepdims=True)) + 1e-06)
    return scaled.astype(jnp.bfloat16)

def reference(queries, keys, values):
    phi_q = feature(queries).reshape(TOKENS, HEADS, HD).transpose(1, 0, 2)
    phi_k = feature(keys).reshape(TOKENS, HEADS, HD).transpose(1, 0, 2)
    vals = values.reshape(TOKENS, HEADS, HD).transpose(1, 0, 2)
    outputs = lax.map(one_head, (phi_q, phi_k, vals))
    return outputs.transpose(1, 0, 2).reshape(TOKENS, HEADS * HD)
```

```python
import functools

import jax
import jax.numpy as jnp
from jax import lax
from jax.experimental import pallas as pl
from jax.experimental.pallas import tpu as pltpu
from jax.sharding import PartitionSpec as P

HEADS = 32
HD = 128
HALF = HEADS // 2
MESH = pl.DeviceIdType.MESH
F32 = jnp.float32
BF16 = jnp.bfloat16


def phi(x):
    x = x.astype(F32)
    return jnp.where(x > 0.0, x + 1.0, jnp.exp(x)).astype(BF16)


def lanes(head, count=1):
    return pl.ds(pl.multiple_of(head * HD, HD), count * HD)


def kernel(
    nx, nz, hp, lag,
    q_hbm, k_hbm, v_hbm, o_hbm,
    qv, kv, vv, kphi, qphi, numer, outv,
    s_par, s_own, e1_recv, t_send, t_recv, z_send, z_recv, q_send, q_recv,
    c_send, c_recv, p_own,
    ld_sem, out_sem, e_ss, e_rs, t_ss, t_rs, z_ss, z_rs, q_ss, q_rs, c_ss, c_rs,
):
    rows = qv.shape[0]
    x = lax.axis_index("head")
    z = lax.axis_index("ctx")
    c = lax.axis_index("sub")
    other = 1 - c

    barrier = pltpu.get_barrier_semaphore()

    def greet(**where):
        pl.semaphore_signal(barrier, inc=1, device_id=where, device_id_type=MESH)

    greet(sub=other)
    for d in range(1, nx):
        greet(head=lax.rem(x + d, nx))

    @pl.when(z > 0)
    def _():
        greet(ctx=z - 1)

    @pl.when(z < nz - 1)
    def _():
        greet(ctx=z + 1)

    def column(u):
        return lax.rem(x + 1 + u, nx)

    def loads(u):
        out = []
        for w in range(2):
            base = (other if w == 0 else c) * HALF + column(u) * hp
            at = lanes(base, hp)
            for m, (src, dst) in enumerate(((k_hbm, kv), (v_hbm, vv))):
                out.append(
                    pltpu.make_async_copy(
                        src.at[:, at], dst.at[:, at], ld_sem.at[u * 4 + w * 2 + m]
                    )
                )
        return out

    for u in range(nx):
        for copy in loads(u):
            copy.start()
    q_load = pltpu.make_async_copy(q_hbm, qv, ld_sem.at[4 * nx])
    q_load.start()

    @pl.when(z == 0)
    def _():
        z_recv[...] = jnp.zeros_like(z_recv)

    def remote(src, dst, ss, rs, **where):
        return pltpu.make_async_remote_copy(
            src_ref=src, dst_ref=dst, send_sem=ss, recv_sem=rs,
            device_id=where, device_id_type=MESH,
        )

    def e_copy(o):
        return remote(s_par.at[o], e1_recv.at[o], e_ss.at[o], e_rs.at[o], sub=other)

    def t_copy(o, col, j):
        return remote(
            t_send.at[o], t_recv.at[x, j], t_ss.at[o], t_rs.at[x * hp + j], head=col
        )

    def t_wait(xs, j):
        remote(
            t_recv.at[xs, j], t_recv.at[xs, j], t_ss.at[0], t_rs.at[xs * hp + j], head=xs
        ).wait_recv()

    def z_copy(j, to):
        return remote(z_send.at[j], z_recv.at[j], z_ss.at[j], z_rs.at[j], ctx=to)

    def q_copy(o, xt, j):
        return remote(
            q_send.at[xt, j], q_recv.at[o], q_ss.at[xt * hp + j], q_rs.at[o], head=xt
        )

    def c_copy(o):
        return remote(c_send.at[o], c_recv.at[o], c_ss.at[o], c_rs.at[o], sub=other)

    up = jnp.where(z < nz - 1, 1, 0)
    down = jnp.where(z > 0, 1, 0)
    pl.semaphore_wait(barrier, nx + up + down)

    def own_index(t):
        u = t // hp
        j = lax.rem(t, hp)
        col = column(u)
        return col * hp + j, col, j

    def first_sums(t):
        o, col, j = own_index(t)
        e_copy(o).wait_recv()
        t_send[o] = (s_own[o].astype(F32) + e1_recv[o].astype(F32)).astype(BF16)
        t_copy(o, col, j).start()

    first_count = (nx - 1) * hp

    def state_step(t, carry):
        o, col, j = own_index(t)
        for u in range(nx):

            @pl.when(t == u * hp)
            def _():
                for copy in loads(u):
                    copy.wait()

        for w in range(2):
            at = lanes((other if w == 0 else c) * HALF + o)
            pk = phi(kv[:, at])
            kphi[:, at] = pk
            s = lax.dot_general(
                pk, vv[:, at], (((0,), (0,)), ((), ())), preferred_element_type=F32
            ).astype(BF16)
            if w == 0:
                s_par[o] = s
            else:
                s_own[o] = s
        e_copy(o).start()

        @pl.when((t >= lag) & (t - lag < first_count))
        def _():
            first_sums(t - lag)

        return carry

    lax.fori_loop(0, HALF, state_step, 0)

    def rest(t, carry):
        first_sums(t)
        return carry

    lax.fori_loop(max(HALF - lag, 0), first_count, rest, 0)

    q_load.wait()
    row = lax.broadcasted_iota(jnp.int32, (rows, rows), 0)
    colm = lax.broadcasted_iota(jnp.int32, (rows, rows), 1)
    causal = row >= colm

    def local_step(g, carry):
        for i in range(4):
            at = lanes(g * 4 + i)
            pq = phi(qv[:, at])
            qphi[:, at] = pq
            scores = lax.dot_general(
                pq, kphi[:, at], (((1,), (1,)), ((), ())), preferred_element_type=F32
            )
            scores = jnp.where(causal, scores, 0.0).astype(BF16)
            numer[:, at] = jnp.dot(scores, vv[:, at], preferred_element_type=F32)
        return carry

    def local_all():
        lax.fori_loop(0, HEADS // 4, local_step, 0)

    early = z >= (nz + 1) // 2

    @pl.when(early)
    def _():
        local_all()

    def deliver(o, before):
        @pl.when(c == 0)
        def _():
            p_own[o] = before.astype(BF16)
            c_send[o] = (before + s_own[o].astype(F32)).astype(BF16)

        @pl.when(c == 1)
        def _():
            c_send[o] = before.astype(BF16)
            p_own[o] = (before + e1_recv[o].astype(F32)).astype(BF16)

        c_copy(o).start()

    def chain(j):
        o = x * hp + j
        e_copy(o).wait_recv()
        t_recv[x, j] = (s_own[o].astype(F32) + e1_recv[o].astype(F32)).astype(BF16)
        for d in range(1, nx):
            t_wait(lax.rem(x + d, nx), j)

        @pl.when(z > 0)
        def _():
            z_copy(j, z - 1).wait_recv()

        @pl.when(z < nz - 1)
        def _():
            total = z_recv[j].astype(F32)
            for xs in range(nx):
                total = total + t_recv[xs, j].astype(F32)
            z_send[j] = total.astype(BF16)
            z_copy(j, z + 1).start()

        for xt in range(nx):

            @pl.when(xt != x)
            def _():
                running = z_recv[j].astype(F32)
                for xs in range(xt):
                    running = running + t_recv[xs, j].astype(F32)
                q_send[xt, j] = running.astype(BF16)
                q_copy(o, xt, j).start()

        for xt in range(nx):

            @pl.when(xt == x)
            def _():
                running = z_recv[j].astype(F32)
                for xs in range(xt):
                    running = running + t_recv[xs, j].astype(F32)
                deliver(o, running)

    def onward(j):
        for d in range(1, nx):
            o = lax.rem(x + d, nx) * hp + j
            q_copy(o, x, j).wait_recv()
            deliver(o, q_recv[o].astype(F32))

    def finish_head(head, prefix):
        at = lanes(head)
        n = numer[:, at] + jnp.dot(qphi[:, at], prefix, preferred_element_type=F32)
        mean = jnp.mean(n * n, axis=-1, keepdims=True)
        outv[:, at] = (n * lax.rsqrt(mean + 1e-06)).astype(BF16)

    def out_copy(head):
        at = lanes(head)
        return pltpu.make_async_copy(outv.at[:, at], o_hbm.at[:, at], out_sem.at[head])

    def finish(j):
        for d in range(nx):
            o = lax.rem(x + d, nx) * hp + j
            finish_head(c * HALF + o, p_own[o])
            out_copy(c * HALF + o).start()
            c_copy(o).wait_recv()
            finish_head(other * HALF + o, c_recv[o])
            out_copy(other * HALF + o).start()

    def relay_step(j, carry):
        chain(j)
        onward(j)

        @pl.when(early & (j > 0))
        def _():
            finish(j - 1)

        return carry

    lax.fori_loop(0, hp, relay_step, 0)

    @pl.when(early)
    def _():
        finish(hp - 1)

    @pl.when(jnp.logical_not(early))
    def _():
        local_all()

        def step(j, carry):
            finish(j)
            return carry

        lax.fori_loop(0, hp, step, 0)

    def drain(o, carry):
        e_copy(o).wait_send()
        c_copy(o).wait_send()
        out_copy(o).wait()
        out_copy(o + HALF).wait()
        return carry

    lax.fori_loop(0, HALF, drain, 0)

    def drain_first(t, carry):
        o, col, j = own_index(t)
        t_copy(o, col, j).wait_send()
        return carry

    lax.fori_loop(0, first_count, drain_first, 0)

    def drain_chain(j, carry):
        @pl.when(z < nz - 1)
        def _():
            z_copy(j, z + 1).wait_send()

        for d in range(1, nx):
            q_copy(x * hp + j, lax.rem(x + d, nx), j).wait_send()
        return carry

    lax.fori_loop(0, hp, drain_chain, 0)


def body(nx, nz, queries, keys, values):
    rows = queries.shape[0]
    hp = HALF // nx
    wide = pltpu.VMEM((rows, HEADS * HD), BF16)
    half = pltpu.VMEM((HALF, HD, HD), BF16)
    dma = pltpu.SemaphoreType.DMA
    return pl.pallas_call(
        functools.partial(kernel, nx, nz, hp, 4),
        out_shape=jax.ShapeDtypeStruct(queries.shape, BF16),
        in_specs=[pl.BlockSpec(memory_space=pl.ANY)] * 3,
        out_specs=pl.BlockSpec(memory_space=pl.ANY),
        scratch_shapes=[
            wide, wide, wide, wide, wide,
            pltpu.VMEM((rows, HEADS * HD), F32),
            wide,
            half, half, half, half,
            pltpu.VMEM((nx, hp, HD, HD), BF16),
            pltpu.VMEM((hp, HD, HD), BF16),
            pltpu.VMEM((hp, HD, HD), BF16),
            pltpu.VMEM((nx, hp, HD, HD), BF16),
            half, half, half, half,
            dma((4 * nx + 1,)), dma((HEADS,)),
            dma((HALF,)), dma((HALF,)),
            dma((HALF,)), dma((HALF,)),
            dma((hp,)), dma((hp,)),
            dma((HALF,)), dma((HALF,)),
            dma((HALF,)), dma((HALF,)),
        ],
        compiler_params=pltpu.CompilerParams(collective_id=0, has_side_effects=True),
    )(queries, keys, values)


def solution(mesh):
    spec = P(("parts", "ctx", "head", "sub"), None)
    return jax.shard_map(
        functools.partial(body, mesh.shape["head"], mesh.shape["ctx"]),
        mesh=mesh,
        in_specs=(spec, spec, spec),
        out_specs=spec,
        check_vma=False,
    )
```

```python
import functools

import jax
import jax.numpy as jnp
from jax import lax
from jax.experimental import pallas as pl
from jax.experimental.pallas import tpu as pltpu
from jax.sharding import PartitionSpec as P

HEADS = 32
HD = 128
HALF = HEADS // 2
MESH = pl.DeviceIdType.MESH
F32 = jnp.float32
BF16 = jnp.bfloat16


def phi(x):
    x = x.astype(F32)
    return jnp.where(x > 0.0, x + 1.0, jnp.exp(x)).astype(BF16)


def lanes(head, count=1):
    return pl.ds(pl.multiple_of(head * HD, HD), count * HD)


def kernel(
    nx, nz, hp, lag, wait_x, wait_c,
    q_hbm, k_hbm, v_hbm, o_hbm,
    qv, kv, vv, kphi, qphi, numer, outv,
    s_par, s_own, e1_recv, t_send, t_recv, z_send, z_recv, q_send, q_recv,
    c_send, c_recv, p_own,
    ld_sem, out_sem, e_ss, e_rs, t_ss, t_rs, z_ss, z_rs, q_ss, q_rs, c_ss, c_rs,
):
    rows = qv.shape[0]
    x = lax.axis_index("head")
    z = lax.axis_index("ctx")
    c = lax.axis_index("sub")
    other = 1 - c

    barrier = pltpu.get_barrier_semaphore()

    def greet(**where):
        pl.semaphore_signal(barrier, inc=1, device_id=where, device_id_type=MESH)

    greet(sub=other)
    for d in range(1, nx):
        greet(head=lax.rem(x + d, nx))

    @pl.when(z > 0)
    def _():
        greet(ctx=z - 1)

    @pl.when(z < nz - 1)
    def _():
        greet(ctx=z + 1)

    def column(u):
        return lax.rem(x + 1 + u, nx)

    def loads(u):
        out = []
        for w in range(2):
            base = (other if w == 0 else c) * HALF + column(u) * hp
            at = lanes(base, hp)
            for m, (src, dst) in enumerate(((k_hbm, kv), (v_hbm, vv))):
                out.append(
                    pltpu.make_async_copy(
                        src.at[:, at], dst.at[:, at], ld_sem.at[u * 4 + w * 2 + m]
                    )
                )
        return out

    for u in range(nx):
        for copy in loads(u):
            copy.start()
    q_load = pltpu.make_async_copy(q_hbm, qv, ld_sem.at[4 * nx])
    q_load.start()

    @pl.when(z == 0)
    def _():
        z_recv[...] = jnp.zeros_like(z_recv)

    def remote(src, dst, ss, rs, **where):
        return pltpu.make_async_remote_copy(
            src_ref=src, dst_ref=dst, send_sem=ss, recv_sem=rs,
            device_id=where, device_id_type=MESH,
        )

    def e_copy(o):
        return remote(s_par.at[o], e1_recv.at[o], e_ss.at[o], e_rs.at[o], sub=other)

    def t_copy(o, col, j):
        return remote(
            t_send.at[o], t_recv.at[x, j], t_ss.at[o], t_rs.at[x * hp + j], head=col
        )

    def t_wait(xs, j):
        remote(
            t_recv.at[xs, j], t_recv.at[xs, j], t_ss.at[0], t_rs.at[xs * hp + j], head=xs
        ).wait_recv()

    def z_copy(j, to):
        return remote(z_send.at[j], z_recv.at[j], z_ss.at[j], z_rs.at[j], ctx=to)

    def q_copy(o, xt, j):
        return remote(
            q_send.at[xt, j], q_recv.at[o], q_ss.at[xt * hp + j], q_rs.at[o], head=xt
        )

    def c_copy(o):
        return remote(c_send.at[o], c_recv.at[o], c_ss.at[o], c_rs.at[o], sub=other)

    up = jnp.where(z < nz - 1, 1, 0)
    down = jnp.where(z > 0, 1, 0)
    pl.semaphore_wait(barrier, nx + up + down)

    def own_index(t):
        u = t // hp
        j = lax.rem(t, hp)
        col = column(u)
        return col * hp + j, col, j

    def first_sums(t):
        o, col, j = own_index(t)
        e_copy(o).wait_recv()
        t_send[o] = (s_own[o].astype(F32) + e1_recv[o].astype(F32)).astype(BF16)
        t_copy(o, col, j).start()

    first_count = (nx - 1) * hp

    def state_step(t, carry):
        o, col, j = own_index(t)
        for u in range(nx):

            @pl.when(t == u * hp)
            def _():
                for copy in loads(u):
                    copy.wait()

        for w in range(2):
            at = lanes((other if w == 0 else c) * HALF + o)
            pk = phi(kv[:, at])
            kphi[:, at] = pk
            s = lax.dot_general(
                pk, vv[:, at], (((0,), (0,)), ((), ())), preferred_element_type=F32
            ).astype(BF16)
            if w == 0:
                s_par[o] = s
            else:
                s_own[o] = s
        e_copy(o).start()

        @pl.when((t >= lag) & (t - lag < first_count))
        def _():
            first_sums(t - lag)

        return carry

    lax.fori_loop(0, HALF, state_step, 0)

    def rest(t, carry):
        first_sums(t)
        return carry

    lax.fori_loop(max(HALF - lag, 0), first_count, rest, 0)

    q_load.wait()
    row = lax.broadcasted_iota(jnp.int32, (rows, rows), 0)
    colm = lax.broadcasted_iota(jnp.int32, (rows, rows), 1)
    causal = row >= colm

    def local_step(g, carry):
        for i in range(4):
            at = lanes(g * 4 + i)
            pq = phi(qv[:, at])
            qphi[:, at] = pq
            scores = lax.dot_general(
                pq, kphi[:, at], (((1,), (1,)), ((), ())), preferred_element_type=F32
            )
            scores = jnp.where(causal, scores, 0.0).astype(BF16)
            numer[:, at] = jnp.dot(scores, vv[:, at], preferred_element_type=F32)
        return carry

    last = z == nz - 1
    groups = HEADS // 4
    before_relay = (groups * z) // max(nz - 1, 1)
    lax.fori_loop(0, before_relay, local_step, 0)

    def deliver(o, before):
        @pl.when(c == 0)
        def _():
            p_own[o] = before.astype(BF16)
            c_send[o] = (before + s_own[o].astype(F32)).astype(BF16)

        @pl.when(c == 1)
        def _():
            c_send[o] = before.astype(BF16)
            p_own[o] = (before + e1_recv[o].astype(F32)).astype(BF16)

        c_copy(o).start()

    def chain(j):
        o = x * hp + j
        e_copy(o).wait_recv()
        t_recv[x, j] = (s_own[o].astype(F32) + e1_recv[o].astype(F32)).astype(BF16)
        for d in range(1, nx):
            t_wait(lax.rem(x + d, nx), j)

        @pl.when(z > 0)
        def _():
            z_copy(j, z - 1).wait_recv()

        @pl.when(z < nz - 1)
        def _():
            total = z_recv[j].astype(F32)
            for xs in range(nx):
                total = total + t_recv[xs, j].astype(F32)
            z_send[j] = total.astype(BF16)
            z_copy(j, z + 1).start()

        for xt in range(nx):

            @pl.when(xt != x)
            def _():
                running = z_recv[j].astype(F32)
                for xs in range(xt):
                    running = running + t_recv[xs, j].astype(F32)
                q_send[xt, j] = running.astype(BF16)
                q_copy(o, xt, j).start()

        for xt in range(nx):

            @pl.when(xt == x)
            def _():
                running = z_recv[j].astype(F32)
                for xs in range(xt):
                    running = running + t_recv[xs, j].astype(F32)
                deliver(o, running)

    def onward(j):
        for d in range(1, nx):
            o = lax.rem(x + d, nx) * hp + j
            q_copy(o, x, j).wait_recv()
            deliver(o, q_recv[o].astype(F32))

    def finish_head(head, prefix):
        at = lanes(head)
        n = numer[:, at] + jnp.dot(qphi[:, at], prefix, preferred_element_type=F32)
        mean = jnp.mean(n * n, axis=-1, keepdims=True)
        outv[:, at] = (n * lax.rsqrt(mean + 1e-06)).astype(BF16)

    def out_copy(head):
        at = lanes(head)
        return pltpu.make_async_copy(outv.at[:, at], o_hbm.at[:, at], out_sem.at[head])

    def finish(j):
        for d in range(nx):
            o = lax.rem(x + d, nx) * hp + j
            finish_head(c * HALF + o, p_own[o])
            out_copy(c * HALF + o).start()
            c_copy(o).wait_recv()
            finish_head(other * HALF + o, c_recv[o])
            out_copy(other * HALF + o).start()

    def relay_step(j, carry):
        @pl.when(j < hp)
        def _():
            chain(j)

        @pl.when((j >= wait_x) & (j < hp + wait_x))
        def _():
            onward(j - wait_x)

        @pl.when(last & (j >= wait_c))
        def _():
            finish(j - wait_c)

        return carry

    lax.fori_loop(0, hp + wait_c, relay_step, 0)

    @pl.when(jnp.logical_not(last))
    def _():
        lax.fori_loop(before_relay, groups, local_step, 0)

        def step(j, carry):
            finish(j)
            return carry

        lax.fori_loop(0, hp, step, 0)

    def drain(o, carry):
        e_copy(o).wait_send()
        c_copy(o).wait_send()
        out_copy(o).wait()
        out_copy(o + HALF).wait()
        return carry

    lax.fori_loop(0, HALF, drain, 0)

    def drain_first(t, carry):
        o, col, j = own_index(t)
        t_copy(o, col, j).wait_send()
        return carry

    lax.fori_loop(0, first_count, drain_first, 0)

    def drain_chain(j, carry):
        @pl.when(z < nz - 1)
        def _():
            z_copy(j, z + 1).wait_send()

        for d in range(1, nx):
            q_copy(x * hp + j, lax.rem(x + d, nx), j).wait_send()
        return carry

    lax.fori_loop(0, hp, drain_chain, 0)


def body(nx, nz, queries, keys, values):
    rows = queries.shape[0]
    hp = HALF // nx
    wide = pltpu.VMEM((rows, HEADS * HD), BF16)
    half = pltpu.VMEM((HALF, HD, HD), BF16)
    dma = pltpu.SemaphoreType.DMA
    return pl.pallas_call(
        functools.partial(kernel, nx, nz, hp, 4, min(3, hp), min(4, hp)),
        out_shape=jax.ShapeDtypeStruct(queries.shape, BF16),
        in_specs=[pl.BlockSpec(memory_space=pl.ANY)] * 3,
        out_specs=pl.BlockSpec(memory_space=pl.ANY),
        scratch_shapes=[
            wide, wide, wide, wide, wide,
            pltpu.VMEM((rows, HEADS * HD), F32),
            wide,
            half, half, half, half,
            pltpu.VMEM((nx, hp, HD, HD), BF16),
            pltpu.VMEM((hp, HD, HD), BF16),
            pltpu.VMEM((hp, HD, HD), BF16),
            pltpu.VMEM((nx, hp, HD, HD), BF16),
            half, half, half, half,
            dma((4 * nx + 1,)), dma((HEADS,)),
            dma((HALF,)), dma((HALF,)),
            dma((HALF,)), dma((HALF,)),
            dma((hp,)), dma((hp,)),
            dma((HALF,)), dma((HALF,)),
            dma((HALF,)), dma((HALF,)),
        ],
        compiler_params=pltpu.CompilerParams(collective_id=0, has_side_effects=True),
    )(queries, keys, values)


def solution(mesh):
    spec = P(("parts", "ctx", "head", "sub"), None)
    return jax.shard_map(
        functools.partial(body, mesh.shape["head"], mesh.shape["ctx"]),
        mesh=mesh,
        in_specs=(spec, spec, spec),
        out_specs=spec,
        check_vma=False,
    )
```

```python
import functools

import jax
import jax.numpy as jnp
from jax import lax
from jax.experimental import pallas as pl
from jax.experimental.pallas import tpu as pltpu
from jax.sharding import PartitionSpec as P

HEADS = 32
HD = 128
HALF = HEADS // 2
MESH = pl.DeviceIdType.MESH
F32 = jnp.float32
BF16 = jnp.bfloat16


def phi(x):
    x = x.astype(F32)
    return jnp.where(x > 0.0, x + 1.0, jnp.exp(x)).astype(BF16)


def lanes(head, count=1):
    return pl.ds(pl.multiple_of(head * HD, HD), count * HD)


def kernel(
    nx, nz, hp, lag, wait_x, wait_c, unroll,
    q_hbm, k_hbm, v_hbm, o_hbm,
    qv, kv, vv, kphi, qphi, numer, outv,
    s_par, s_own, e1_recv, t_send, t_recv, z_send, z_recv, q_send, q_recv,
    c_send, c_recv, p_own,
    ld_sem, out_sem, e_ss, e_rs, t_ss, t_rs, z_ss, z_rs, q_ss, q_rs, c_ss, c_rs,
):
    rows = qv.shape[0]
    x = lax.axis_index("head")
    z = lax.axis_index("ctx")
    c = lax.axis_index("sub")
    other = 1 - c

    barrier = pltpu.get_barrier_semaphore()

    def greet(**where):
        pl.semaphore_signal(barrier, inc=1, device_id=where, device_id_type=MESH)

    greet(sub=other)
    for d in range(1, nx):
        greet(head=lax.rem(x + d, nx))

    @pl.when(z > 0)
    def _():
        greet(ctx=z - 1)

    @pl.when(z < nz - 1)
    def _():
        greet(ctx=z + 1)

    def column(u):
        return lax.rem(x + 1 + u, nx)

    def loads(u):
        out = []
        for w in range(2):
            base = (other if w == 0 else c) * HALF + column(u) * hp
            at = lanes(base, hp)
            for m, (src, dst) in enumerate(((k_hbm, kv), (v_hbm, vv))):
                out.append(
                    pltpu.make_async_copy(
                        src.at[:, at], dst.at[:, at], ld_sem.at[u * 4 + w * 2 + m]
                    )
                )
        return out

    for u in range(nx):
        for copy in loads(u):
            copy.start()
    q_load = pltpu.make_async_copy(q_hbm, qv, ld_sem.at[4 * nx])
    q_load.start()

    @pl.when(z == 0)
    def _():
        z_recv[...] = jnp.zeros_like(z_recv)

    def remote(src, dst, ss, rs, **where):
        return pltpu.make_async_remote_copy(
            src_ref=src, dst_ref=dst, send_sem=ss, recv_sem=rs,
            device_id=where, device_id_type=MESH,
        )

    def e_copy(o):
        return remote(s_par.at[o], e1_recv.at[o], e_ss.at[o], e_rs.at[o], sub=other)

    def t_copy(o, col, j):
        return remote(
            t_send.at[o], t_recv.at[x, j], t_ss.at[o], t_rs.at[x * hp + j], head=col
        )

    def t_wait(xs, j):
        remote(
            t_recv.at[xs, j], t_recv.at[xs, j], t_ss.at[0], t_rs.at[xs * hp + j], head=xs
        ).wait_recv()

    def z_copy(j, to):
        return remote(z_send.at[j], z_recv.at[j], z_ss.at[j], z_rs.at[j], ctx=to)

    def q_copy(o, xt, j):
        return remote(
            q_send.at[xt, j], q_recv.at[o], q_ss.at[xt * hp + j], q_rs.at[o], head=xt
        )

    def c_copy(o):
        return remote(c_send.at[o], c_recv.at[o], c_ss.at[o], c_rs.at[o], sub=other)

    up = jnp.where(z < nz - 1, 1, 0)
    down = jnp.where(z > 0, 1, 0)
    pl.semaphore_wait(barrier, nx + up + down)

    def own_index(t):
        u = t // hp
        j = lax.rem(t, hp)
        col = column(u)
        return col * hp + j, col, j

    def first_sums(t):
        o, col, j = own_index(t)
        e_copy(o).wait_recv()
        t_send[o] = (s_own[o].astype(F32) + e1_recv[o].astype(F32)).astype(BF16)
        t_copy(o, col, j).start()

    first_count = (nx - 1) * hp

    def state_step(t, carry):
        o, col, j = own_index(t)
        for u in range(nx):

            @pl.when(t == u * hp)
            def _():
                for copy in loads(u):
                    copy.wait()

        for w in range(2):
            at = lanes((other if w == 0 else c) * HALF + o)
            pk = phi(kv[:, at])
            kphi[:, at] = pk
            s = lax.dot_general(
                pk, vv[:, at], (((0,), (0,)), ((), ())), preferred_element_type=F32
            ).astype(BF16)
            if w == 0:
                s_par[o] = s
            else:
                s_own[o] = s
        e_copy(o).start()

        @pl.when((t >= lag) & (t - lag < first_count))
        def _():
            first_sums(t - lag)

        return carry

    lax.fori_loop(0, HALF, state_step, 0)

    def rest(t, carry):
        first_sums(t)
        return carry

    lax.fori_loop(max(HALF - lag, 0), first_count, rest, 0)

    q_load.wait()
    row = lax.broadcasted_iota(jnp.int32, (rows, rows), 0)
    colm = lax.broadcasted_iota(jnp.int32, (rows, rows), 1)
    causal = row >= colm

    def local_step(g, carry):
        for i in range(unroll):
            at = lanes(g * unroll + i)
            pq = phi(qv[:, at])
            qphi[:, at] = pq
            scores = lax.dot_general(
                pq, kphi[:, at], (((1,), (1,)), ((), ())), preferred_element_type=F32
            )
            scores = jnp.where(causal, scores, 0.0).astype(BF16)
            numer[:, at] = jnp.dot(scores, vv[:, at], preferred_element_type=F32)
        return carry

    last = z == nz - 1
    groups = HEADS // unroll
    before_relay = (groups * z) // max(nz - 1, 1)
    lax.fori_loop(0, before_relay, local_step, 0)

    def deliver(o, before):
        @pl.when(c == 0)
        def _():
            p_own[o] = before.astype(BF16)
            c_send[o] = (before + s_own[o].astype(F32)).astype(BF16)

        @pl.when(c == 1)
        def _():
            c_send[o] = before.astype(BF16)
            p_own[o] = (before + e1_recv[o].astype(F32)).astype(BF16)

        c_copy(o).start()

    def chain(j):
        o = x * hp + j
        e_copy(o).wait_recv()
        t_recv[x, j] = (s_own[o].astype(F32) + e1_recv[o].astype(F32)).astype(BF16)
        for d in range(1, nx):
            t_wait(lax.rem(x + d, nx), j)

        @pl.when(z > 0)
        def _():
            z_copy(j, z - 1).wait_recv()

        @pl.when(z < nz - 1)
        def _():
            total = z_recv[j].astype(F32)
            for xs in range(nx):
                total = total + t_recv[xs, j].astype(F32)
            z_send[j] = total.astype(BF16)
            z_copy(j, z + 1).start()

    def back(j):
        o = x * hp + j
        for xt in range(nx):

            @pl.when(xt != x)
            def _():
                running = z_recv[j].astype(F32)
                for xs in range(xt):
                    running = running + t_recv[xs, j].astype(F32)
                q_send[xt, j] = running.astype(BF16)
                q_copy(o, xt, j).start()

        for xt in range(nx):

            @pl.when(xt == x)
            def _():
                running = z_recv[j].astype(F32)
                for xs in range(xt):
                    running = running + t_recv[xs, j].astype(F32)
                deliver(o, running)

    def onward(j):
        for d in range(1, nx):
            o = lax.rem(x + d, nx) * hp + j
            q_copy(o, x, j).wait_recv()
            deliver(o, q_recv[o].astype(F32))

    def finish_head(head, prefix):
        at = lanes(head)
        n = numer[:, at] + jnp.dot(qphi[:, at], prefix, preferred_element_type=F32)
        mean = jnp.mean(n * n, axis=-1, keepdims=True)
        outv[:, at] = (n * lax.rsqrt(mean + 1e-06)).astype(BF16)

    def out_copy(head):
        at = lanes(head)
        return pltpu.make_async_copy(outv.at[:, at], o_hbm.at[:, at], out_sem.at[head])

    def finish(j):
        heads = []
        for d in range(nx):
            o = lax.rem(x + d, nx) * hp + j
            c_copy(o).wait_recv()
            heads.append((c * HALF + o, o, p_own))
            heads.append((other * HALF + o, o, c_recv))
        for head, o, held in heads:
            finish_head(head, held[o])
        for head, o, held in heads:
            out_copy(head).start()

    def relay_step(j, carry):
        chain(j)

        @pl.when(z > 0)
        def _():
            back(j)

        @pl.when(last & (j >= wait_x))
        def _():
            onward(j - wait_x)

        @pl.when(last & (j >= wait_c))
        def _():
            finish(j - wait_c)

        return carry

    lax.fori_loop(0, hp, relay_step, 0)

    @pl.when(z == 0)
    def _():
        def back_step(j, carry):
            back(j)
            return carry

        lax.fori_loop(0, hp, back_step, 0)

    lax.fori_loop(before_relay, groups, local_step, 0)

    def final_step(j, carry):
        @pl.when(j < hp + wait_x)
        def _():
            onward(j - wait_x)

        @pl.when(j >= wait_c)
        def _():
            finish(j - wait_c)

        return carry

    lax.fori_loop(jnp.where(last, hp, wait_x), hp + wait_c, final_step, 0)

    def drain(o, carry):
        e_copy(o).wait_send()
        c_copy(o).wait_send()
        out_copy(o).wait()
        out_copy(o + HALF).wait()
        return carry

    lax.fori_loop(0, HALF, drain, 0)

    def drain_first(t, carry):
        o, col, j = own_index(t)
        t_copy(o, col, j).wait_send()
        return carry

    lax.fori_loop(0, first_count, drain_first, 0)

    def drain_chain(j, carry):
        @pl.when(z < nz - 1)
        def _():
            z_copy(j, z + 1).wait_send()

        for d in range(1, nx):
            q_copy(x * hp + j, lax.rem(x + d, nx), j).wait_send()
        return carry

    lax.fori_loop(0, hp, drain_chain, 0)


def body(nx, nz, queries, keys, values):
    rows = queries.shape[0]
    hp = HALF // nx
    wide = pltpu.VMEM((rows, HEADS * HD), BF16)
    half = pltpu.VMEM((HALF, HD, HD), BF16)
    dma = pltpu.SemaphoreType.DMA
    return pl.pallas_call(
        functools.partial(kernel, nx, nz, hp, 4, min(4, hp), min(7, hp), 4),
        out_shape=jax.ShapeDtypeStruct(queries.shape, BF16),
        in_specs=[pl.BlockSpec(memory_space=pl.ANY)] * 3,
        out_specs=pl.BlockSpec(memory_space=pl.ANY),
        scratch_shapes=[
            wide, wide, wide, wide, wide,
            pltpu.VMEM((rows, HEADS * HD), F32),
            wide,
            half, half, half, half,
            pltpu.VMEM((nx, hp, HD, HD), BF16),
            pltpu.VMEM((hp, HD, HD), BF16),
            pltpu.VMEM((hp, HD, HD), BF16),
            pltpu.VMEM((nx, hp, HD, HD), BF16),
            half, half, half, half,
            dma((4 * nx + 1,)), dma((HEADS,)),
            dma((HALF,)), dma((HALF,)),
            dma((HALF,)), dma((HALF,)),
            dma((hp,)), dma((hp,)),
            dma((HALF,)), dma((HALF,)),
            dma((HALF,)), dma((HALF,)),
        ],
        compiler_params=pltpu.CompilerParams(collective_id=0, has_side_effects=True),
    )(queries, keys, values)


def solution(mesh):
    spec = P(("parts", "ctx", "head", "sub"), None)
    return jax.shard_map(
        functools.partial(body, mesh.shape["head"], mesh.shape["ctx"]),
        mesh=mesh,
        in_specs=(spec, spec, spec),
        out_specs=spec,
        check_vma=False,
    )
```

```python
import functools

import jax
import jax.numpy as jnp
from jax import lax
from jax.experimental import pallas as pl
from jax.experimental.pallas import tpu as pltpu
from jax.sharding import PartitionSpec as P

HEADS = 32
HD = 128
HALF = HEADS // 2
MESH = pl.DeviceIdType.MESH
F32 = jnp.float32
BF16 = jnp.bfloat16


def phi(x):
    x = x.astype(F32)
    return jnp.where(x > 0.0, x + 1.0, jnp.exp(x)).astype(BF16)


def lanes(head, count=1):
    return pl.ds(pl.multiple_of(head * HD, HD), count * HD)


def kernel(
    nx, nz, hp, lag, wait_x, wait_c, unroll,
    q_hbm, k_hbm, v_hbm, o_hbm,
    qv, kv, vv, kphi, qphi, numer, outv,
    s_par, s_own, e1_recv, t_send, t_recv, z_send, z_recv, q_send, q_recv,
    c_send, c_recv, p_own,
    ld_sem, out_sem, e_ss, e_rs, t_ss, t_rs, z_ss, z_rs, q_ss, q_rs, c_ss, c_rs,
):
    rows = qv.shape[0]
    x = lax.axis_index("head")
    z = lax.axis_index("ctx")
    c = lax.axis_index("sub")
    other = 1 - c

    barrier = pltpu.get_barrier_semaphore()

    def greet(**where):
        pl.semaphore_signal(barrier, inc=1, device_id=where, device_id_type=MESH)

    greet(sub=other)
    for d in range(1, nx):
        greet(head=lax.rem(x + d, nx))

    @pl.when(z > 0)
    def _():
        greet(ctx=z - 1)

    @pl.when(z < nz - 1)
    def _():
        greet(ctx=z + 1)

    def column(u):
        return lax.rem(x + 1 + u, nx)

    def loads(u):
        out = []
        for w in range(2):
            base = (other if w == 0 else c) * HALF + column(u) * hp
            at = lanes(base, hp)
            for m, (src, dst) in enumerate(((k_hbm, kv), (v_hbm, vv))):
                out.append(
                    pltpu.make_async_copy(
                        src.at[:, at], dst.at[:, at], ld_sem.at[u * 4 + w * 2 + m]
                    )
                )
        return out

    for u in range(nx):
        for copy in loads(u):
            copy.start()
    q_load = pltpu.make_async_copy(q_hbm, qv, ld_sem.at[4 * nx])
    q_load.start()

    @pl.when(z == 0)
    def _():
        z_recv[...] = jnp.zeros_like(z_recv)

    def remote(src, dst, ss, rs, **where):
        return pltpu.make_async_remote_copy(
            src_ref=src, dst_ref=dst, send_sem=ss, recv_sem=rs,
            device_id=where, device_id_type=MESH,
        )

    def e_copy(o):
        return remote(s_par.at[o], e1_recv.at[o], e_ss.at[o], e_rs.at[o], sub=other)

    def t_copy(o, col, j):
        return remote(
            t_send.at[o], t_recv.at[x, j], t_ss.at[o], t_rs.at[x * hp + j], head=col
        )

    def t_wait(xs, j):
        remote(
            t_recv.at[xs, j], t_recv.at[xs, j], t_ss.at[0], t_rs.at[xs * hp + j], head=xs
        ).wait_recv()

    def z_copy(j, to):
        return remote(z_send.at[j], z_recv.at[j], z_ss.at[j], z_rs.at[j], ctx=to)

    def q_copy(o, xt, j):
        return remote(
            q_send.at[xt, j], q_recv.at[o], q_ss.at[xt * hp + j], q_rs.at[o], head=xt
        )

    def c_copy(o):
        return remote(c_send.at[o], c_recv.at[o], c_ss.at[o], c_rs.at[o], sub=other)

    up = jnp.where(z < nz - 1, 1, 0)
    down = jnp.where(z > 0, 1, 0)
    pl.semaphore_wait(barrier, nx + up + down)

    def own_index(t):
        u = t // hp
        j = lax.rem(t, hp)
        col = column(u)
        return col * hp + j, col, j

    def first_sums(t):
        o, col, j = own_index(t)
        e_copy(o).wait_recv()
        t_send[o] = (s_own[o].astype(F32) + e1_recv[o].astype(F32)).astype(BF16)
        t_copy(o, col, j).start()

    first_count = (nx - 1) * hp

    def state_step(t, carry):
        o, col, j = own_index(t)
        for u in range(nx):

            @pl.when(t == u * hp)
            def _():
                for copy in loads(u):
                    copy.wait()

        for w in range(2):
            at = lanes((other if w == 0 else c) * HALF + o)
            pk = phi(kv[:, at])
            kphi[:, at] = pk
            s = lax.dot_general(
                pk, vv[:, at], (((0,), (0,)), ((), ())), preferred_element_type=F32
            ).astype(BF16)
            if w == 0:
                s_par[o] = s
            else:
                s_own[o] = s
        e_copy(o).start()

        @pl.when((t >= lag) & (t - lag < first_count))
        def _():
            first_sums(t - lag)

        return carry

    lax.fori_loop(0, HALF, state_step, 0)

    def rest(t, carry):
        first_sums(t)
        return carry

    lax.fori_loop(max(HALF - lag, 0), first_count, rest, 0)

    q_load.wait()
    row = lax.broadcasted_iota(jnp.int32, (rows, rows), 0)
    colm = lax.broadcasted_iota(jnp.int32, (rows, rows), 1)
    causal = row >= colm

    def local_step(g, carry):
        for i in range(unroll):
            at = lanes(g * unroll + i)
            pq = phi(qv[:, at])
            qphi[:, at] = pq
            scores = lax.dot_general(
                pq, kphi[:, at], (((1,), (1,)), ((), ())), preferred_element_type=F32
            )
            scores = jnp.where(causal, scores, 0.0).astype(BF16)
            numer[:, at] = jnp.dot(scores, vv[:, at], preferred_element_type=F32)
        return carry

    last = z == nz - 1
    groups = HEADS // unroll
    before_relay = (groups * z) // max(nz - 1, 1)
    lax.fori_loop(0, before_relay, local_step, 0)

    def deliver(o, before):
        @pl.when(c == 0)
        def _():
            p_own[o] = before.astype(BF16)
            c_send[o] = (before + s_own[o].astype(F32)).astype(BF16)

        @pl.when(c == 1)
        def _():
            c_send[o] = before.astype(BF16)
            p_own[o] = (before + e1_recv[o].astype(F32)).astype(BF16)

        c_copy(o).start()

    def chain(j):
        o = x * hp + j
        e_copy(o).wait_recv()
        t_recv[x, j] = (s_own[o].astype(F32) + e1_recv[o].astype(F32)).astype(BF16)
        for d in range(1, nx):
            t_wait(lax.rem(x + d, nx), j)

        @pl.when(z > 0)
        def _():
            z_copy(j, z - 1).wait_recv()

        @pl.when(z < nz - 1)
        def _():
            total = z_recv[j].astype(F32)
            for xs in range(nx):
                total = total + t_recv[xs, j].astype(F32)
            z_send[j] = total.astype(BF16)
            z_copy(j, z + 1).start()

    def back(j):
        o = x * hp + j
        for xt in range(nx):

            @pl.when(xt != x)
            def _():
                running = z_recv[j].astype(F32)
                for xs in range(xt):
                    running = running + t_recv[xs, j].astype(F32)
                q_send[xt, j] = running.astype(BF16)
                q_copy(o, xt, j).start()

        for xt in range(nx):

            @pl.when(xt == x)
            def _():
                running = z_recv[j].astype(F32)
                for xs in range(xt):
                    running = running + t_recv[xs, j].astype(F32)
                deliver(o, running)

    def onward(j):
        for d in range(1, nx):
            o = lax.rem(x + d, nx) * hp + j
            q_copy(o, x, j).wait_recv()
            deliver(o, q_recv[o].astype(F32))

    def finish_head(head, prefix):
        at = lanes(head)
        n = numer[:, at] + jnp.dot(qphi[:, at], prefix, preferred_element_type=F32)
        mean = jnp.mean(n * n, axis=-1, keepdims=True)
        outv[:, at] = (n * lax.rsqrt(mean + 1e-06)).astype(BF16)

    def out_copy(head):
        at = lanes(head)
        return pltpu.make_async_copy(outv.at[:, at], o_hbm.at[:, at], out_sem.at[head])

    def finish(j):
        heads = []
        for d in range(nx):
            o = lax.rem(x + d, nx) * hp + j
            c_copy(o).wait_recv()
            heads.append((c * HALF + o, o, p_own))
            heads.append((other * HALF + o, o, c_recv))
        for head, o, held in heads:
            finish_head(head, held[o])
        for head, o, held in heads:
            out_copy(head).start()

    def relay_step(j, carry):
        chain(j)

        @pl.when(z > 0)
        def _():
            back(j)

        @pl.when(last & (j >= wait_x))
        def _():
            onward(j - wait_x)

        @pl.when(last & (j >= wait_c))
        def _():
            finish(j - wait_c)

        return carry

    lax.fori_loop(0, hp, relay_step, 0)

    @pl.when(z == 0)
    def _():
        def back_step(j, carry):
            back(j)
            return carry

        lax.fori_loop(0, hp, back_step, 0)

    lax.fori_loop(before_relay, groups, local_step, 0)

    def final_step(j, carry):
        @pl.when(j < hp + wait_x)
        def _():
            onward(j - wait_x)

        @pl.when(j >= wait_c)
        def _():
            finish(j - wait_c)

        return carry

    lax.fori_loop(jnp.where(last, hp, wait_x), hp + wait_c, final_step, 0)

    def drain(o, carry):
        e_copy(o).wait_send()
        c_copy(o).wait_send()
        out_copy(o).wait()
        out_copy(o + HALF).wait()
        return carry

    lax.fori_loop(0, HALF, drain, 0)

    def drain_first(t, carry):
        o, col, j = own_index(t)
        t_copy(o, col, j).wait_send()
        return carry

    lax.fori_loop(0, first_count, drain_first, 0)

    def drain_chain(j, carry):
        @pl.when(z < nz - 1)
        def _():
            z_copy(j, z + 1).wait_send()

        for d in range(1, nx):
            q_copy(x * hp + j, lax.rem(x + d, nx), j).wait_send()
        return carry

    lax.fori_loop(0, hp, drain_chain, 0)


def body(nx, nz, queries, keys, values):
    rows = queries.shape[0]
    hp = HALF // nx
    wide = pltpu.VMEM((rows, HEADS * HD), BF16)
    half = pltpu.VMEM((HALF, HD, HD), BF16)
    dma = pltpu.SemaphoreType.DMA
    return pl.pallas_call(
        functools.partial(kernel, nx, nz, hp, 4, min(5, hp), min(8, hp), 4),
        out_shape=jax.ShapeDtypeStruct(queries.shape, BF16),
        in_specs=[pl.BlockSpec(memory_space=pl.ANY)] * 3,
        out_specs=pl.BlockSpec(memory_space=pl.ANY),
        scratch_shapes=[
            wide, wide, wide, wide, wide,
            pltpu.VMEM((rows, HEADS * HD), F32),
            wide,
            half, half, half, half,
            pltpu.VMEM((nx, hp, HD, HD), BF16),
            pltpu.VMEM((hp, HD, HD), BF16),
            pltpu.VMEM((hp, HD, HD), BF16),
            pltpu.VMEM((nx, hp, HD, HD), BF16),
            half, half, half, half,
            dma((4 * nx + 1,)), dma((HEADS,)),
            dma((HALF,)), dma((HALF,)),
            dma((HALF,)), dma((HALF,)),
            dma((hp,)), dma((hp,)),
            dma((HALF,)), dma((HALF,)),
            dma((HALF,)), dma((HALF,)),
        ],
        compiler_params=pltpu.CompilerParams(collective_id=0, has_side_effects=True),
    )(queries, keys, values)


def solution(mesh):
    spec = P(("parts", "ctx", "head", "sub"), None)
    return jax.shard_map(
        functools.partial(body, mesh.shape["head"], mesh.shape["ctx"]),
        mesh=mesh,
        in_specs=(spec, spec, spec),
        out_specs=spec,
        check_vma=False,
    )
```
